32 devices in a mesh: row: 8 (over z, y), col: 4 (over x, core).
Axes of the slice: x: 2, y: 2, z: 4, core: 2. Of those that a mesh axis runs over, the one named last changes fastest.
Arguments:
- residual: float32 [512, 512, 256], P('row', 'col'), may hold values from -6 to 6
- adjoint: float32 [512, 512, 256], P('row', 'col'), may hold values from -6 to 6
- coefficient: bfloat16 [512, 512, 256], P('row', 'col'), may hold values from 0.25 to 4
- basis_x: float32 [512, 512], replicated, may hold values from -0.25 to 0.25
- basis_y: float32 [512, 512], replicated, may hold values from -0.25 to 0.25
- basis_z: float32 [256, 256], replicated, may hold values from -0.375 to 0.375
- eigen_x: float32 [512], replicated, may hold values from 0.02 to 2
- eigen_y: float32 [512], replicated, may hold values from 0.02 to 2
- eigen_z: float32 [256], replicated, may hold values from 0.02 to 2
Outputs:
- adjoint_next: float32 [512, 512, 256], P('row', 'col')
- residual_next: float32 [512, 512, 256], P('row', 'col')
The draws below stay inside these ranges and needn't reach their ends.
All inputs are finite; a program needn't handle non-finite values.
Results may differ from the reference program's by a relative error of at most 0.0003.
Values sent between devices are 32-bit elements; how exact they have to be, the bound alone decides.
No kernel may reach another device: no remote copies, remote signals or barrier semaphores. Data moves between devices by JAX's collectives and lax.ppermute only.
A program may use at most 192 MiB of HBM per device.

```python
import math
import jax
import jax.numpy as jnp
from jax import lax

NX = 512
NY = 512
NZ = 256


def shard_levels(own_key, extent, split, low, high):
    def one(dim, blocks):
        steps = jax.random.uniform(jax.random.fold_in(jax.random.fold_in(own_key, 6), dim), (blocks,), jnp.float32, low / len(split), high / len(split))
        return jnp.repeat(jnp.exp(steps), extent[dim] // blocks).reshape((-1,) + (1,) * (len(extent) - dim - 1))

    level = one(*split[0])
    for cut in split[1:]:
        level = level * one(*cut)
    return level


def bell_draw(own_key, dims, width, reach, pieces=(), kind=jnp.bfloat16):
    level = shard_levels(own_key, dims, pieces, -0.22, 0.18) if pieces else 1.0
    array = jax.random.normal(own_key, dims, jnp.float32) * width * level
    return jnp.minimum(jnp.maximum(array, -reach), reach).astype(kind)


def setup_inputs(seed: int = 0) -> dict:
    key_of = jax.random.split(jax.random.key(seed), 10)
    return {
        "residual": bell_draw(key_of[0], (NX, NY, NZ), 1.0, 6.0, ((0, 8), (1, 4)), jnp.float32),
        "adjoint": bell_draw(key_of[1], (NX, NY, NZ), 1.0, 6.0, ((0, 8), (1, 4)), jnp.float32),
        "coefficient": jnp.clip(jnp.exp(math.log(4.0) - 2.7725887 * jax.random.uniform(key_of[2], (NX, NY, NZ), jnp.float32) ** shard_levels(key_of[2], (NX, NY, NZ), ((0, 8), (1, 4)), -0.2, 0.2)), 0.25, 4.0).astype(jnp.bfloat16),
        "basis_x": bell_draw(key_of[3], (NX, NX), NX ** -0.5, 0.25, (), jnp.float32),
        "basis_y": bell_draw(key_of[4], (NY, NY), NY ** -0.5, 0.25, (), jnp.float32),
        "basis_z": bell_draw(key_of[5], (NZ, NZ), NZ ** -0.5, 0.375, (), jnp.float32),
        "eigen_x": jnp.clip(jnp.exp(jax.random.uniform(key_of[6], (NX,), jnp.float32, math.log(0.02), math.log(2.0))), 0.02, 2.0),
        "eigen_y": jnp.clip(jnp.exp(jax.random.uniform(key_of[7], (NY,), jnp.float32, math.log(0.02), math.log(2.0))), 0.02, 2.0),
        "eigen_z": jnp.clip(jnp.exp(jax.random.uniform(key_of[8], (NZ,), jnp.float32, math.log(0.02), math.log(2.0))), 0.02, 2.0),
    }


MASS_TAPS = (1.0 / 5040, 120.0 / 5040, 1191.0 / 5040, 2416.0 / 5040, 1191.0 / 5040, 120.0 / 5040, 1.0 / 5040)
STIFF_TAPS = (-1.0 / 120, -0.2, -0.125, 2.0 / 3.0, -0.125, -0.2, -1.0 / 120)


def taps_along(padded, coeffs, axis_dim, length):
    running = coeffs[0] * lax.slice_in_dim(padded, 0, length, axis=axis_dim)
    for offset in range(1, 7):
        running = running + coeffs[offset] * lax.slice_in_dim(padded, offset, offset + length, axis=axis_dim)
    return running


def stiffness(padded, length_x, length_y, length_z):
    mass_x = taps_along(padded, MASS_TAPS, 0, length_x)
    stiff_x = taps_along(padded, STIFF_TAPS, 0, length_x)
    mass_xy = taps_along(mass_x, MASS_TAPS, 1, length_y)
    stiff_y = taps_along(mass_x, STIFF_TAPS, 1, length_y)
    stiff_xm = taps_along(stiff_x, MASS_TAPS, 1, length_y)
    return taps_along(stiff_y + stiff_xm, MASS_TAPS, 2, length_z) + taps_along(mass_xy, STIFF_TAPS, 2, length_z)


def reference(residual, adjoint, coefficient, basis_x, basis_y, basis_z, eigen_x, eigen_y, eigen_z):
    highest = lax.Precision.HIGHEST
    spectrum = jnp.einsum('xyz,zc->xyc', residual, basis_z, precision=highest)
    spectrum = jnp.einsum('xyc,yb->xbc', spectrum, basis_y, precision=highest)
    spectrum = jnp.einsum('xbc,xa->abc', spectrum, basis_x, precision=highest)
    denominator = eigen_x[:, None, None] + eigen_y[None, :, None] + eigen_z[None, None, :]
    scaled = spectrum / denominator
    correction = jnp.einsum('abc,xa->xbc', scaled, basis_x, precision=highest)
    correction = jnp.einsum('xbc,yb->xyc', correction, basis_y, precision=highest)
    correction = jnp.einsum('xyc,zc->xyz', correction, basis_z, precision=highest)
    weighted = coefficient.astype(jnp.float32) * correction
    padded = jnp.pad(weighted, 3)
    image = stiffness(padded, NX, NY, NZ)
    return adjoint + correction, residual - image
```

```python
import jax
import jax.numpy as jnp
import numpy as np
from jax import lax
from jax.experimental import pallas as pl
from jax.experimental.pallas import tpu as pltpu
from jax.sharding import PartitionSpec as P


MASS = tuple(t / 5040 for t in (1.0, 120.0, 1191.0, 2416.0, 1191.0, 120.0, 1.0))
STIFF = (-1.0 / 120, -0.2, -0.125, 2.0 / 3.0, -0.125, -0.2, -1.0 / 120)
F32, BF16 = jnp.float32, jnp.bfloat16
NN = (((1,), (0,)), ((), ()))
NT = (((1,), (1,)), ((), ()))
TN = (((0,), (0,)), ((), ()))


def params(n, limit=56 << 20):
    return pltpu.CompilerParams(
        dimension_semantics=("arbitrary",) * n, vmem_limit_bytes=limit
    )


def cost(flops, nbytes):
    return pl.CostEstimate(flops=flops, bytes_accessed=nbytes, transcendentals=0)


def split(v):
    high = v.astype(BF16)
    return high, (v - high.astype(F32)).astype(BF16)


def split_outside(v):
    high = lax.reduce_precision(v, 8, 7)
    return high.astype(BF16), (v - high).astype(BF16)


def dot3(a, b, dims):
    def dot(p, q):
        return lax.dot_general(p, q, dims, preferred_element_type=F32)

    return dot(a[0], b[0]) + (dot(a[0], b[1]) + dot(a[1], b[0]))


def join(parts, axis):
    return parts[0] if len(parts) == 1 else jnp.concatenate(parts, axis=axis)


def sum_dots(parts, mat, dims_width):
    if dims_width % 128 == 0:
        a = (join([p[0] for p in parts], 1), join([p[1] for p in parts], 1))
        return dot3(a, (mat[0][...], mat[1][...]), NN)
    total = None
    for e, p in enumerate(parts):
        rows = pl.ds(e * dims_width, dims_width)
        term = dot3(p, (mat[0][rows, :], mat[1][rows, :]), NN)
        total = term if total is None else total + term
    return total


def whole(shape):
    return pl.BlockSpec(shape, lambda *_: (0,) * len(shape))


def forward_z(residual, basis_zt, where, chunks, peers, part):
    nx, ny, nz = residual.shape
    xb = 8
    group = peers * part

    def kernel(where_ref, r_ref, b_ref, *outs):
        me = where_ref[0]
        rows = [
            b_ref[pl.ds(pl.multiple_of(k * group + (me ^ d) * part, part), part), :]
            for k in chunks
            for d in range(peers)
        ]
        basis = split(join(rows, 0))
        for x in range(xb):
            t = dot3(basis, split(r_ref[x]), NT)
            for n, out in enumerate(outs):
                out[x] = t[n * part : (n + 1) * part, :]

    count = len(chunks) * peers
    outs = pl.pallas_call(
        kernel,
        grid_spec=pltpu.PrefetchScalarGridSpec(
            num_scalar_prefetch=1,
            grid=(nx // xb,),
            in_specs=[
                pl.BlockSpec((xb, ny, nz), lambda i, w: (i, 0, 0)),
                pl.BlockSpec(basis_zt.shape, lambda i, w: (0, 0)),
            ],
            out_specs=[pl.BlockSpec((xb, part, ny), lambda i, w: (i, 0, 0))] * count,
        ),
        out_shape=[jax.ShapeDtypeStruct((nx, part, ny), F32)] * count,
        compiler_params=params(1),
        cost_estimate=cost(6 * nx * ny * nz * len(chunks) * group, nx * ny * nz * 4),
        name="forward_z",
    )(where, residual, basis_zt)
    return [outs[n * peers : (n + 1) * peers] for n in range(len(chunks))]


def forward_x(pieces, bxt, peers, after):
    nx, part, ny = pieces[0].shape
    full = nx * len(pieces)
    wide = full // peers

    def kernel(_, bh, bl, *refs):
        ins, outs = refs[: len(pieces)], refs[len(pieces) :]

        def step(c):
            v = split(join([r[:, c, :] for r in ins], 0))
            t = dot3((bh[...], bl[...]), v, NN)
            for e, out in enumerate(outs):
                out[c] = t[e * wide : (e + 1) * wide, :]
            return 0

        for c in range(part):
            step(c)

    return pl.pallas_call(
        kernel,
        out_shape=[jax.ShapeDtypeStruct((part, wide, ny), F32)] * peers,
        in_specs=[pl.BlockSpec(memory_space=pl.ANY)]
        + [pl.BlockSpec(memory_space=pltpu.VMEM)] * (2 + len(pieces)),
        out_specs=[pl.BlockSpec(memory_space=pltpu.VMEM)] * peers,
        compiler_params=params(0),
        cost_estimate=cost(6 * full * full * part * ny, 8 * full * part * ny),
        name="forward_x",
    )(after, *bxt, *pieces)


def middle_y(pieces, by, byt, shift, eigen_y, after):
    part, wide, ny = pieces[0].shape
    peers = len(pieces)
    full = peers * ny
    cb = 2 if part % 2 == 0 and wide % 8 == 0 else 1

    def kernel(_, bh, bl, th, tl, shift_ref, ey_ref, *refs):
        ins, outs = refs[:peers], refs[peers:]
        parts = [split(r[...].reshape(cb * wide, ny)) for r in ins]
        spectrum = sum_dots(parts, (bh, bl), ny)
        ey = ey_ref[...]
        scaled = [
            spectrum[n * wide : (n + 1) * wide, :] / (shift_ref[n] + ey)
            for n in range(cb)
        ]
        back = dot3(split(join(scaled, 0)), (th[...], tl[...]), NN)
        for e, out in enumerate(outs):
            out[...] = back[:, e * ny : (e + 1) * ny].reshape(cb, wide, ny)

    spec = pl.BlockSpec((cb, wide, ny), lambda i: (i, 0, 0))
    return pl.pallas_call(
        kernel,
        grid=(part // cb,),
        out_shape=[jax.ShapeDtypeStruct((part, wide, ny), F32)] * peers,
        in_specs=[pl.BlockSpec(memory_space=pl.ANY)]
        + [whole((full, full))] * 4
        + [pl.BlockSpec((cb, wide, 1), lambda i: (i, 0, 0)), whole((1, full))]
        + [spec] * peers,
        out_specs=[spec] * peers,
        compiler_params=params(1),
        cost_estimate=cost(12 * full * full * part * wide, 8 * full * part * wide),
        name="middle_y",
    )(after, *by, *byt, shift, eigen_y, *pieces)


def backward_x(pieces, bx, peers, after):
    part, wide, ny = pieces[0].shape
    full = wide * len(pieces)
    nx = full // peers

    def kernel(_, bh, bl, *refs):
        ins, outs = refs[: len(pieces)], refs[len(pieces) :]
        for c in range(part):
            v = split(join([r[c] for r in ins], 0))
            t = dot3((bh[...], bl[...]), v, NN)
            for d, out in enumerate(outs):
                out[:, c, :] = t[d * nx : (d + 1) * nx, :]

    return pl.pallas_call(
        kernel,
        out_shape=[jax.ShapeDtypeStruct((nx, part, ny), F32)] * peers,
        in_specs=[pl.BlockSpec(memory_space=pl.ANY)]
        + [pl.BlockSpec(memory_space=pltpu.VMEM)] * (2 + len(pieces)),
        out_specs=[pl.BlockSpec(memory_space=pltpu.VMEM)] * peers,
        compiler_params=params(0),
        cost_estimate=cost(6 * full * full * part * ny, 8 * full * part * ny),
        name="backward_x",
    )(after, *bx, *pieces)


def backward_z(pieces, basis_zt, where, adjoint, coefficient):
    nx, ny, nz = adjoint.shape
    peers, part = len(pieces[0]), pieces[0][0].shape[1]
    group = peers * part
    chunks = len(pieces)
    xb = 8
    flat = [p for chunk in pieces for p in chunk]

    def kernel(where_ref, b_ref, adj_ref, coef_ref, *refs):
        ins, (next_ref, weighted_ref) = refs[:-2], refs[-2:]
        me = where_ref[0]
        rows = [
            b_ref[pl.ds(pl.multiple_of(k * group + (me ^ d) * part, part), part), :]
            for k in range(chunks)
            for d in range(peers)
        ]
        basis = split(join(rows, 0))
        for x in range(xb):
            v = split(join([r[x] for r in ins], 0))
            correction = dot3(v, basis, TN)
            next_ref[x] = adj_ref[x] + correction
            weighted_ref[x] = coef_ref[x].astype(F32) * correction

    field = pl.BlockSpec((xb, ny, nz), lambda i, w: (i, 0, 0))
    return pl.pallas_call(
        kernel,
        grid_spec=pltpu.PrefetchScalarGridSpec(
            num_scalar_prefetch=1,
            grid=(nx // xb,),
            in_specs=[pl.BlockSpec(basis_zt.shape, lambda i, w: (0, 0)), field, field]
            + [pl.BlockSpec((xb, part, ny), lambda i, w: (i, 0, 0))] * len(flat),
            out_specs=[field, field],
        ),
        out_shape=[jax.ShapeDtypeStruct((nx, ny, nz), F32)] * 2,
        compiler_params=params(1),
        cost_estimate=cost(6 * nx * ny * nz * nz, 22 * nx * ny * nz),
        name="backward_z",
    )(where, basis_zt, adjoint, coefficient, *flat)


def band(n):
    out = np.zeros((2 * n, n), np.float32)
    for j in range(-3, 4):
        out[:n] += MASS[j + 3] * np.eye(n, k=j, dtype=np.float32)
        out[n:] += STIFF[j + 3] * np.eye(n, k=j, dtype=np.float32)
    return out


def taps(load, mass=True, stiff=True):
    mid = load(0)
    pair = [load(j) + load(-j) for j in (1, 2, 3)]
    out = []
    for use, co in ((mass, MASS), (stiff, STIFF)):
        if use:
            out.append(co[3] * mid + co[4] * pair[0] + co[5] * pair[1] + co[6] * pair[2])
    return out


def stencil(weighted, residual, x_low, x_high, y_low, y_high, bands):
    nx, ny, nz = weighted.shape
    xb = 8
    steps = nx // xb
    halves = nz // 128

    def kernel(bh, bl, xl, xh, yl, yh, prev, cur, nxt, r_ref, out, ps, qs, ph, qh):
        i = pl.program_id(0)

        @pl.when(i == 0)
        def _():
            for side, ref in ((0, yl), (1, yh)):
                for j in range(3):
                    p, q = taps(lambda o: ref[j, 3 + o : 3 + o + nx, :])
                    ph[side, :, j, :] = p
                    qh[side, :, j, :] = q

        first, last = i == 0, i == steps - 1
        before = [
            jnp.where(first, xl[j], prev[xb - 3 + j]) for j in range(3)
        ]
        after = [jnp.where(last, xh[j], nxt[j]) for j in range(3)]

        for x in range(xb):

            def plane(o):
                n = x + o
                if n < 0:
                    return before[n + 3]
                return cur[n] if n < xb else after[n - xb]

            p, q = taps(plane)
            for h in range(halves):
                cols = slice(h * 128, (h + 1) * 128)
                ps[h, 8 : 8 + ny, :] = p[:, cols]
                qs[h, 8 : 8 + ny, :] = q[:, cols]
                for side, base in ((0, 5), (1, 8 + ny)):
                    ps[h, base : base + 3, :] = ph[side, i * xb + x, :3, cols]
                    qs[h, base : base + 3, :] = qh[side, i * xb + x, :3, cols]
            first_terms, second_terms = [], []
            for h in range(halves):
                mp, kp = taps(lambda o: ps[h, 8 + o : 8 + o + ny, :])
                (mq,) = taps(lambda o: qs[h, 8 + o : 8 + o + ny, :], stiff=False)
                first_terms.append(kp + mq)
                second_terms.append(mp)
            both = split(join(first_terms + second_terms, 1))
            out[x] = r_ref[x] - dot3(both, (bh[...], bl[...]), NN)

    field = pl.BlockSpec((xb, ny, nz), lambda i: (i, 0, 0))
    return pl.pallas_call(
        kernel,
        grid=(steps,),
        in_specs=[whole(b.shape) for b in bands]
        + [whole(x_low.shape)] * 2
        + [whole(y_low.shape)] * 2
        + [
            pl.BlockSpec((xb, ny, nz), lambda i: (jnp.maximum(i - 1, 0), 0, 0)),
            field,
            pl.BlockSpec((xb, ny, nz), lambda i: (jnp.minimum(i + 1, steps - 1), 0, 0)),
            field,
        ],
        out_specs=field,
        out_shape=jax.ShapeDtypeStruct((nx, ny, nz), F32),
        scratch_shapes=[pltpu.VMEM((halves, ny + 16, 128), F32)] * 2
        + [pltpu.VMEM((2, nx, 8, nz), F32)] * 2,
        compiler_params=params(1),
        cost_estimate=cost(12 * nx * ny * nz * nz, 12 * nx * ny * nz),
        name="stencil",
    )(*bands, x_low, x_high, y_low, y_high, weighted, weighted, weighted, residual)


def exchange(pieces, axis):
    n = len(pieces)
    out = [pieces[0]] + [None] * (n - 1)
    for d in range(n - 1, 0, -1):
        out[d] = lax.ppermute(pieces[d], axis, [(i, i ^ d) for i in range(n)])
    return out


def neighbours(low, high, axis):
    n = lax.axis_size(axis)
    up = [(i, i + 1) for i in range(n - 1)]
    down = [(i + 1, i) for i in range(n - 1)]
    return lax.ppermute(high, axis, up), lax.ppermute(low, axis, down)


def schedule(chunks):
    order = [("z", 0), ("z", 1)][:chunks]
    if chunks == 4:
        order += [("x", 0), ("y", 0), ("b", 0), ("x", 1), ("x", 2), ("y", 1)]
        order += [("x", 3), ("y", 2), ("b", 1), ("y", 3), ("b", 2), ("b", 3)]
    else:
        order += [(s, k) for k in range(chunks) for s in ("x", "y", "b")]
    return order


def chunk_count(nz, rows):
    return max(1, min(4, nz // (rows * 8)))


def shards(residual, adjoint, coefficient, basis_x, basis_y, basis_z, eigen_x, eigen_y, eigen_z):
    nx, ny, nz = residual.shape
    rows, cols = lax.axis_size("row"), lax.axis_size("col")
    ri, ci = lax.axis_index("row"), lax.axis_index("col")
    width_x = nx * rows
    wide = width_x // cols
    chunks = chunk_count(nz, rows)
    part = nz // (rows * chunks)
    where = jnp.stack([ri, ci]).astype(jnp.int32)

    basis_zt = basis_z.T
    bx = jnp.concatenate(
        [lax.dynamic_slice_in_dim(basis_x, (ri ^ d) * nx, nx, 0) for d in range(rows)], 0
    )
    bx = jnp.concatenate(
        [lax.dynamic_slice_in_dim(bx, (ci ^ e) * wide, wide, 1) for e in range(cols)], 1
    )
    by = jnp.concatenate(
        [lax.dynamic_slice_in_dim(basis_y, (ci ^ e) * ny, ny, 0) for e in range(cols)], 0
    )
    bx2, by2 = split_outside(bx), split_outside(by)
    bxt2, byt2 = tuple(b.T for b in bx2), tuple(b.T for b in by2)
    ex = lax.dynamic_slice_in_dim(eigen_x, ci * wide, wide)
    ez = lax.dynamic_slice_in_dim(eigen_z.reshape(chunks, rows, part), ri, 1, 1)[:, 0]
    shift = (ez[:, :, None] + ex[None, None, :])[..., None]
    ey = eigen_y[None, :]
    bands = split_outside(jnp.asarray(band(nz)))

    fw, mid, ret, back = ([None] * chunks for _ in range(4))
    last = where
    for stage, k in schedule(chunks):
        if stage == "z":
            these = (k,) if k == 0 else tuple(range(k, chunks))
            outs = forward_z(residual, basis_zt, where, these, rows, part)
            for n, out in zip(these, outs):
                fw[n] = (out, "row")
            last = outs[-1][0]
        elif stage == "x":
            out = forward_x(fw[k], bxt2, cols, last)
        elif stage == "y":
            out = middle_y(mid[k], by2, byt2, shift[k], ey, last)
        else:
            out = backward_x(ret[k], bx2, rows, last)
        if stage == "z":
            for n in these:
                fw[n] = exchange(*fw[n])
        elif stage == "x":
            mid[k] = exchange(out, "col")
        elif stage == "y":
            ret[k] = exchange(out, "col")
        else:
            back[k] = exchange(out, "row")
        if stage != "z":
            last = out[0]
    adjoint_next, weighted = backward_z(back, basis_zt, where, adjoint, coefficient)
    x_low, x_high = neighbours(weighted[:3], weighted[-3:], "row")
    edge_low = jnp.concatenate([x_low[:, :3], weighted[:, :3], x_high[:, :3]], 0)
    edge_high = jnp.concatenate([x_low[:, -3:], weighted[:, -3:], x_high[:, -3:]], 0)
    y_low, y_high = neighbours(
        edge_low.transpose(1, 0, 2), edge_high.transpose(1, 0, 2), "col"
    )
    residual_next = stencil(weighted, residual, x_low, x_high, y_low, y_high, bands)
    return adjoint_next, residual_next


def solution(mesh):
    field = P("row", "col", None)
    return jax.shard_map(
        shards,
        mesh=mesh,
        in_specs=(field,) * 3 + (P(),) * 6,
        out_specs=(field, field),
        check_vma=False,
    )
```

```python
import jax
import jax.numpy as jnp
import numpy as np
from jax import lax
from jax.experimental import pallas as pl
from jax.experimental.pallas import tpu as pltpu
from jax.sharding import PartitionSpec as P


MASS = tuple(t / 5040 for t in (1.0, 120.0, 1191.0, 2416.0, 1191.0, 120.0, 1.0))
STIFF = (-1.0 / 120, -0.2, -0.125, 2.0 / 3.0, -0.125, -0.2, -1.0 / 120)
F32, BF16 = jnp.float32, jnp.bfloat16
NN = (((1,), (0,)), ((), ()))
NT = (((1,), (1,)), ((), ()))
TN = (((0,), (0,)), ((), ()))


def params(n, limit=56 << 20):
    return pltpu.CompilerParams(
        dimension_semantics=("arbitrary",) * n, vmem_limit_bytes=limit
    )


def cost(flops, nbytes):
    return pl.CostEstimate(flops=flops, bytes_accessed=nbytes, transcendentals=0)


def split(v):
    high = v.astype(BF16)
    return high, (v - high.astype(F32)).astype(BF16)


def split_outside(v):
    high = lax.reduce_precision(v, 8, 7)
    return high.astype(BF16), (v - high).astype(BF16)


def dot3(a, b, dims):
    def dot(p, q):
        return lax.dot_general(p, q, dims, preferred_element_type=F32)

    return dot(a[0], b[0]) + (dot(a[0], b[1]) + dot(a[1], b[0]))


def join(parts, axis):
    return parts[0] if len(parts) == 1 else jnp.concatenate(parts, axis=axis)


def sum_dots(parts, mat, dims_width):
    if dims_width % 128 == 0:
        a = (join([p[0] for p in parts], 1), join([p[1] for p in parts], 1))
        return dot3(a, (mat[0][...], mat[1][...]), NN)
    total = None
    for e, p in enumerate(parts):
        rows = pl.ds(e * dims_width, dims_width)
        term = dot3(p, (mat[0][rows, :], mat[1][rows, :]), NN)
        total = term if total is None else total + term
    return total


def pairwise(a, v, i):
    ny = v.shape[2]
    if ny % 128:
        return [(c, dot3(a, split(v[c]), NN)) for c in (2 * i, 2 * i + 1)]
    t = dot3(a, split(join([v[2 * i], v[2 * i + 1]], 1)), NN)
    return [(2 * i, t[:, :ny]), (2 * i + 1, t[:, ny:])]


def whole(shape):
    return pl.BlockSpec(shape, lambda *_: (0,) * len(shape))


def forward_z(residual, basis_zt, where, chunks, peers, part):
    nx, ny, nz = residual.shape
    xb = 8
    group = peers * part

    def kernel(where_ref, r_ref, b_ref, *outs):
        me = where_ref[0]
        rows = [
            b_ref[pl.ds(pl.multiple_of(k * group + (me ^ d) * part, part), part), :]
            for k in chunks
            for d in range(peers)
        ]
        basis = split(join(rows, 0))

        for x in range(xb):
            t = dot3(basis, split(r_ref[x]), NT)
            for n, out in enumerate(outs):
                out[x] = t[n * part : (n + 1) * part, :]

    count = len(chunks) * peers
    outs = pl.pallas_call(
        kernel,
        grid_spec=pltpu.PrefetchScalarGridSpec(
            num_scalar_prefetch=1,
            grid=(nx // xb,),
            in_specs=[
                pl.BlockSpec((xb, ny, nz), lambda i, w: (i, 0, 0)),
                pl.BlockSpec(basis_zt.shape, lambda i, w: (0, 0)),
            ],
            out_specs=[pl.BlockSpec((xb, part, ny), lambda i, w: (i, 0, 0))] * count,
        ),
        out_shape=[jax.ShapeDtypeStruct((nx, part, ny), F32)] * count,
        compiler_params=params(1),
        cost_estimate=cost(6 * nx * ny * nz * len(chunks) * group, nx * ny * nz * 4),
        name="forward_z",
    )(where, residual, basis_zt)
    return [outs[n * peers : (n + 1) * peers] for n in range(len(chunks))]


def forward_x(pieces, bxt, peers, after):
    nx, part, ny = pieces[0].shape
    full = nx * len(pieces)
    wide = full // peers

    def kernel(_, bh, bl, *refs):
        ins, outs, v = refs[: len(pieces)], refs[len(pieces) : -1], refs[-1]
        for c in range(part):
            for d, r in enumerate(ins):
                v[c, d * nx : (d + 1) * nx, :] = r[:, c, :]

        @pl.loop(0, part // 2)
        def _(i):
            for c, t in pairwise((bh[...], bl[...]), v, i):
                for e, out in enumerate(outs):
                    out[c] = t[e * wide : (e + 1) * wide, :]

    return pl.pallas_call(
        kernel,
        out_shape=[jax.ShapeDtypeStruct((part, wide, ny), F32)] * peers,
        in_specs=[pl.BlockSpec(memory_space=pl.ANY)]
        + [pl.BlockSpec(memory_space=pltpu.VMEM)] * (2 + len(pieces)),
        out_specs=[pl.BlockSpec(memory_space=pltpu.VMEM)] * peers,
        compiler_params=params(0),
        cost_estimate=cost(6 * full * full * part * ny, 8 * full * part * ny),
        scratch_shapes=[pltpu.VMEM((part, full, ny), F32)],
        name="forward_x",
    )(after, *bxt, *pieces)


def middle_y(pieces, by, byt, shift, eigen_y, after):
    part, wide, ny = pieces[0].shape
    peers = len(pieces)
    full = peers * ny
    cb = 2 if part % 2 == 0 and wide % 8 == 0 else 1

    def kernel(_, bh, bl, th, tl, shift_ref, ey_ref, *refs):
        ins, outs = refs[:peers], refs[peers:]
        parts = [split(r[...].reshape(cb * wide, ny)) for r in ins]
        spectrum = sum_dots(parts, (bh, bl), ny)
        ey = ey_ref[...]
        scaled = [
            spectrum[n * wide : (n + 1) * wide, :] / (shift_ref[n] + ey)
            for n in range(cb)
        ]
        back = dot3(split(join(scaled, 0)), (th[...], tl[...]), NN)
        for e, out in enumerate(outs):
            out[...] = back[:, e * ny : (e + 1) * ny].reshape(cb, wide, ny)

    spec = pl.BlockSpec((cb, wide, ny), lambda i: (i, 0, 0))
    return pl.pallas_call(
        kernel,
        grid=(part // cb,),
        out_shape=[jax.ShapeDtypeStruct((part, wide, ny), F32)] * peers,
        in_specs=[pl.BlockSpec(memory_space=pl.ANY)]
        + [whole((full, full))] * 4
        + [pl.BlockSpec((cb, wide, 1), lambda i: (i, 0, 0)), whole((1, full))]
        + [spec] * peers,
        out_specs=[spec] * peers,
        compiler_params=params(1),
        cost_estimate=cost(12 * full * full * part * wide, 8 * full * part * wide),
        name="middle_y",
    )(after, *by, *byt, shift, eigen_y, *pieces)


def backward_x(pieces, bx, peers, after):
    part, wide, ny = pieces[0].shape
    full = wide * len(pieces)
    nx = full // peers

    def kernel(_, bh, bl, *refs):
        ins, outs, v, w = refs[: len(pieces)], refs[len(pieces) : -2], refs[-2], refs[-1]
        for n, r in enumerate(ins):
            v[:, n * wide : (n + 1) * wide, :] = r[...]

        @pl.loop(0, part // 2)
        def _(i):
            for c, t in pairwise((bh[...], bl[...]), v, i):
                w[c] = t

        for c in range(part):
            for d, out in enumerate(outs):
                out[:, c, :] = w[c, d * nx : (d + 1) * nx, :]

    return pl.pallas_call(
        kernel,
        out_shape=[jax.ShapeDtypeStruct((nx, part, ny), F32)] * peers,
        in_specs=[pl.BlockSpec(memory_space=pl.ANY)]
        + [pl.BlockSpec(memory_space=pltpu.VMEM)] * (2 + len(pieces)),
        out_specs=[pl.BlockSpec(memory_space=pltpu.VMEM)] * peers,
        compiler_params=params(0),
        cost_estimate=cost(6 * full * full * part * ny, 8 * full * part * ny),
        scratch_shapes=[pltpu.VMEM((part, full, ny), F32)] * 2,
        name="backward_x",
    )(after, *bx, *pieces)


def backward_z(pieces, basis_zt, where, adjoint, coefficient):
    nx, ny, nz = adjoint.shape
    peers, part = len(pieces[0]), pieces[0][0].shape[1]
    group = peers * part
    chunks = len(pieces)
    xb = 8
    steps = nx // xb
    flat = [p for chunk in pieces for p in chunk]

    def kernel(where_ref, b_ref, adj_ref, coef_ref, *refs):
        ins, (next_ref, w_ref, *slabs_edges) = refs[: len(flat)], refs[len(flat) :]
        slabs, edges = slabs_edges[:2], slabs_edges[2:]
        me, i = where_ref[0], pl.program_id(0)
        rows = [
            b_ref[pl.ds(pl.multiple_of(k * group + (me ^ d) * part, part), part), :]
            for k in range(chunks)
            for d in range(peers)
        ]
        basis = split(join(rows, 0))

        for x in range(xb):
            v = split(join([r[x] for r in ins], 0))
            correction = dot3(v, basis, TN)
            next_ref[x] = adj_ref[x] + correction
            w_ref[x] = coef_ref[x].astype(F32) * correction

        for n in range(2):

            @pl.when(where_ref[1] % 2 == n)
            def _():
                for j in range(3):
                    edges[n][j] = w_ref[:, ny - 3 + j, :]
                    edges[1 - n][j] = w_ref[:, j, :]

            @pl.when((i == 0) & (me % 2 == n))
            def _():
                slabs[1 - n][...] = w_ref[:3]

            @pl.when((i == steps - 1) & (me % 2 == n))
            def _():
                slabs[n][...] = w_ref[xb - 3 :]

    field = pl.BlockSpec((xb, ny, nz), lambda i, w: (i, 0, 0))
    slab = pl.BlockSpec((3, ny, nz), lambda i, w: (0, 0, 0))
    edge = pl.BlockSpec((3, xb, nz), lambda i, w: (0, i, 0))
    shapes = [(nx, ny, nz)] * 2 + [(3, ny, nz)] * 2 + [(3, nx, nz)] * 2
    return pl.pallas_call(
        kernel,
        grid_spec=pltpu.PrefetchScalarGridSpec(
            num_scalar_prefetch=1,
            grid=(steps,),
            in_specs=[pl.BlockSpec(basis_zt.shape, lambda i, w: (0, 0)), field, field]
            + [pl.BlockSpec((xb, part, ny), lambda i, w: (i, 0, 0))] * len(flat),
            out_specs=[field] * 2 + [slab] * 2 + [edge] * 2,
        ),
        out_shape=[jax.ShapeDtypeStruct(shape, F32) for shape in shapes],
        compiler_params=params(1),
        cost_estimate=cost(6 * nx * ny * nz * nz, 22 * nx * ny * nz),
        name="backward_z",
    )(where, basis_zt, adjoint, coefficient, *flat)


def band(n):
    out = np.zeros((2 * n, n), np.float32)
    for j in range(-3, 4):
        out[:n] += MASS[j + 3] * np.eye(n, k=j, dtype=np.float32)
        out[n:] += STIFF[j + 3] * np.eye(n, k=j, dtype=np.float32)
    return out


def taps(load, mass=True, stiff=True):
    mid = load(0)
    pair = [load(j) + load(-j) for j in (1, 2, 3)]
    out = []
    for use, co in ((mass, MASS), (stiff, STIFF)):
        if use:
            out.append(co[3] * mid + co[4] * pair[0] + co[5] * pair[1] + co[6] * pair[2])
    return out


def stencil(weighted, residual, bands, halos=None, after=None):
    nx, ny, nz = weighted.shape
    xb = 8
    steps = nx // xb
    halves = nz // 128
    outer = halos is not None
    rows = lax.axis_size("row")

    def kernel(_, bh, bl, *refs):
        i = pl.program_id(0)
        if outer:
            where_ref, xa, xc, prev, cur, nxt, r_ref, out, win, ps, qs = refs
        else:
            prev, cur, nxt, r_ref, out, win, ps, qs = refs

        @pl.when(i == 0)
        def _():
            zero = jnp.zeros((halves, 8, 128), F32)
            for ref in (ps, qs):
                ref[:, :8, :] = zero
                ref[:, 8 + ny :, :] = zero

        win[:3] = prev[xb - 3 :]
        win[3 : 3 + xb] = cur[...]
        win[3 + xb :] = nxt[:3]
        if outer:
            me = where_ref[0]

            @pl.when(i == 0)
            def _():
                low = jnp.where(me % 2 == 0, xc[...], xa[...])
                win[:3] = jnp.where(me == 0, 0.0, low)

            @pl.when(i == 1)
            def _():
                high = jnp.where(me % 2 == 0, xa[...], xc[...])
                win[3 + xb :] = jnp.where(me == rows - 1, 0.0, high)

        @pl.loop(0, xb)
        def _(x):
            p, q = taps(lambda o: win[x + 3 + o])
            for h in range(halves):
                cols = slice(h * 128, (h + 1) * 128)
                ps[h, 8 : 8 + ny, :] = p[:, cols]
                qs[h, 8 : 8 + ny, :] = q[:, cols]
            first_terms, second_terms = [], []
            for h in range(halves):
                mp, kp = taps(lambda o: ps[h, 8 + o : 8 + o + ny, :])
                (mq,) = taps(lambda o: qs[h, 8 + o : 8 + o + ny, :], stiff=False)
                first_terms.append(kp + mq)
                second_terms.append(mp)
            both = split(join(first_terms + second_terms, 1))
            out[x] = r_ref[x] - dot3(both, (bh[...], bl[...]), NN)

    if outer:
        at = lambda i: i * (steps - 1)
        count = 2
    else:
        at = lambda i: i + 1
        count = steps - 2

    def block(shift):
        return pl.BlockSpec(
            (xb, ny, nz),
            lambda i: (jnp.clip(at(i) + shift, 0, steps - 1), 0, 0),
        )

    extra = list(halos) if outer else []
    return pl.pallas_call(
        kernel,
        grid=(count,),
        in_specs=[pl.BlockSpec(memory_space=pl.ANY)]
        + [whole(b.shape) for b in bands]
        + ([pl.BlockSpec(memory_space=pltpu.SMEM)] if outer else [])
        + [whole(e.shape) for e in extra[1:]]
        + [block(-1), block(0), block(1), block(0)],
        out_specs=block(0),
        out_shape=jax.ShapeDtypeStruct((nx, ny, nz), F32),
        scratch_shapes=[pltpu.VMEM((xb + 6, ny, nz), F32)]
        + [pltpu.VMEM((halves, ny + 16, 128), F32)] * 2,
        input_output_aliases={0: 0} if outer else {},
        compiler_params=params(1),
        cost_estimate=cost(12 * count * xb * ny * nz * nz, 12 * count * xb * ny * nz),
        name="stencil_outer" if outer else "stencil_inner",
    )(weighted if after is None else after, *bands, *extra, weighted, weighted, weighted, residual)


def stencil_sides(partial, where, bands, edges, corners):
    nx, ny, nz = partial.shape

    rows, cols = lax.axis_size("row"), lax.axis_size("col")

    def kernel(where_ref, bh, bl, ea, ec, ca, cc, r_ref, out, ext, ph, qh):
        me, mine = where_ref[0], where_ref[1]
        for side in range(2):

            @pl.when(pl.program_id(0) == side)
            def _():
                ph[...] = jnp.zeros_like(ph)
                qh[...] = jnp.zeros_like(qh)
                base = 5 if side == 0 else 16
                near = mine % 2 == 1 - side
                pick = jnp.where(near, 0, 1)
                border = mine == (0 if side == 0 else cols - 1)
                for j in range(3):
                    edge = jnp.where(near, ea[j], ec[j])
                    even = me % 2 == 0
                    low = jnp.where(even, cc[pick, j], ca[pick, j])
                    high = jnp.where(even, ca[pick, j], cc[pick, j])
                    ext[:8] = jnp.where(border | (me == 0), 0.0, low)
                    ext[8 : 8 + nx] = jnp.where(border, 0.0, edge)
                    ext[8 + nx :] = jnp.where(border | (me == rows - 1), 0.0, high)
                    p, q = taps(lambda o: ext[8 + o : 8 + o + nx, :])
                    ph[:, base + j, :] = p
                    qh[:, base + j, :] = q

        mp, kp = taps(lambda o: ph[:, 8 + o : 16 + o, :])
        (mq,) = taps(lambda o: qh[:, 8 + o : 16 + o, :], stiff=False)
        both = split(jnp.concatenate([kp + mq, mp], 2).reshape(nx * 8, 2 * nz))
        image = dot3(both, (bh[...], bl[...]), NN)
        out[...] = r_ref[...] - image.reshape(nx, 8, nz)

    field = pl.BlockSpec((nx, 8, nz), lambda i: (0, i * (ny // 8 - 1), 0))
    return pl.pallas_call(
        kernel,
        grid=(2,),
        in_specs=[pl.BlockSpec(memory_space=pltpu.SMEM)]
        + [whole(b.shape) for b in bands]
        + [whole(e.shape) for e in edges]
        + [whole(c.shape) for c in corners]
        + [field],
        out_specs=field,
        out_shape=jax.ShapeDtypeStruct((nx, ny, nz), F32),
        scratch_shapes=[pltpu.VMEM((nx + 16, nz), F32)]
        + [pltpu.VMEM((nx, 24, nz), F32)] * 2,
        input_output_aliases={7: 0},
        compiler_params=params(1),
        cost_estimate=cost(12 * nx * 16 * nz * nz, 128 * nx * nz),
        name="stencil_sides",
    )(where, *bands, *edges, *corners, partial)


def exchange(pieces, axis):
    n = len(pieces)
    out = [pieces[0]] + [None] * (n - 1)
    for d in range(n - 1, 0, -1):
        out[d] = lax.ppermute(pieces[d], axis, [(i, i ^ d) for i in range(n)])
    return out


def swap(array, axis, near):
    n = lax.axis_size(axis)
    other = [i ^ 1 if near else (i + 1 if i % 2 else i - 1) for i in range(n)]
    return lax.ppermute(
        array, axis, [(i, j if 0 <= j < n else i) for i, j in enumerate(other)]
    )


def schedule(chunks):
    order = [("z", 0), ("z", 1)][:chunks]
    if chunks == 4:
        order += [("x", 0), ("y", 0), ("b", 0), ("x", 1), ("x", 2), ("y", 1)]
        order += [("x", 3), ("y", 2), ("b", 1), ("y", 3), ("b", 2), ("b", 3)]
    else:
        order += [(s, k) for k in range(chunks) for s in ("x", "y", "b")]
    return order


def chunk_count(nz, rows):
    return max(1, min(4, nz // (rows * 8)))


def shards(residual, adjoint, coefficient, basis_x, basis_y, basis_z, eigen_x, eigen_y, eigen_z):
    nx, ny, nz = residual.shape
    rows, cols = lax.axis_size("row"), lax.axis_size("col")
    ri, ci = lax.axis_index("row"), lax.axis_index("col")
    width_x = nx * rows
    wide = width_x // cols
    chunks = chunk_count(nz, rows)
    part = nz // (rows * chunks)
    where = jnp.stack([ri, ci]).astype(jnp.int32)

    basis_zt = basis_z.T
    bx = jnp.concatenate(
        [lax.dynamic_slice_in_dim(basis_x, (ri ^ d) * nx, nx, 0) for d in range(rows)], 0
    )
    bx = jnp.concatenate(
        [lax.dynamic_slice_in_dim(bx, (ci ^ e) * wide, wide, 1) for e in range(cols)], 1
    )
    by = jnp.concatenate(
        [lax.dynamic_slice_in_dim(basis_y, (ci ^ e) * ny, ny, 0) for e in range(cols)], 0
    )
    bx2, by2 = split_outside(bx), split_outside(by)
    bxt2, byt2 = tuple(b.T for b in bx2), tuple(b.T for b in by2)
    ex = lax.dynamic_slice_in_dim(eigen_x, ci * wide, wide)
    ez = lax.dynamic_slice_in_dim(eigen_z.reshape(chunks, rows, part), ri, 1, 1)[:, 0]
    shift = (ez[:, :, None] + ex[None, None, :])[..., None]
    ey = eigen_y[None, :]
    bands = split_outside(jnp.asarray(band(nz)))

    fw, mid, ret, back = ([None] * chunks for _ in range(4))
    last = where
    for stage, k in schedule(chunks):
        if stage == "z":
            these = (k,) if k == 0 else tuple(range(k, chunks))
            outs = forward_z(residual, basis_zt, where, these, rows, part)
            for n, out in zip(these, outs):
                fw[n] = (out, "row")
            last = outs[-1][0]
        elif stage == "x":
            out = forward_x(fw[k], bxt2, cols, last)
        elif stage == "y":
            out = middle_y(mid[k], by2, byt2, shift[k], ey, last)
        else:
            out = backward_x(ret[k], bx2, rows, last)
        if stage == "z":
            for n in these:
                fw[n] = exchange(*fw[n])
        elif stage == "x":
            mid[k] = exchange(out, "col")
        elif stage == "y":
            ret[k] = exchange(out, "col")
        else:
            back[k] = exchange(out, "row")
        if stage != "z":
            last = out[0]
    adjoint_next, weighted, xa, xc, ea, ec = backward_z(
        back, basis_zt, where, adjoint, coefficient
    )
    ea, ec = swap(ea, "col", True), swap(ec, "col", False)
    xa, xc = swap(xa, "row", True), swap(xc, "row", False)
    inner = stencil(weighted, residual, bands)
    sides, _ = lax.optimization_barrier((jnp.stack([ea, ec]), inner))
    low, high = sides[:, :, :8], sides[:, :, -8:]
    even = ri % 2 == 0
    ca = swap(jnp.where(even, high, low), "row", True)
    cc = swap(jnp.where(even, low, high), "row", False)
    outer = stencil(weighted, residual, bands, (where, xa, xc), inner)
    residual_next = stencil_sides(outer, where, bands, (ea, ec), (ca, cc))
    return adjoint_next, residual_next


def solution(mesh):
    field = P("row", "col", None)
    return jax.shard_map(
        shards,
        mesh=mesh,
        in_specs=(field,) * 3 + (P(),) * 6,
        out_specs=(field, field),
        check_vma=False,
    )
```

```python
import jax
import jax.numpy as jnp
import numpy as np
from jax import lax
from jax.experimental import pallas as pl
from jax.experimental.pallas import tpu as pltpu
from jax.sharding import PartitionSpec as P


MASS = tuple(t / 5040 for t in (1.0, 120.0, 1191.0, 2416.0, 1191.0, 120.0, 1.0))
STIFF = (-1.0 / 120, -0.2, -0.125, 2.0 / 3.0, -0.125, -0.2, -1.0 / 120)
F32, BF16 = jnp.float32, jnp.bfloat16
NN = (((1,), (0,)), ((), ()))
NT = (((1,), (1,)), ((), ()))
TN = (((0,), (0,)), ((), ()))


def params(n, limit=56 << 20):
    return pltpu.CompilerParams(
        dimension_semantics=("arbitrary",) * n, vmem_limit_bytes=limit
    )


def cost(flops, nbytes):
    return pl.CostEstimate(flops=flops, bytes_accessed=nbytes, transcendentals=0)


def split(v):
    high = v.astype(BF16)
    return high, (v - high.astype(F32)).astype(BF16)


def split_outside(v):
    high = lax.reduce_precision(v, 8, 7)
    return high.astype(BF16), (v - high).astype(BF16)


def dot3(a, b, dims):
    def dot(p, q):
        return lax.dot_general(p, q, dims, preferred_element_type=F32)

    return dot(a[0], b[0]) + (dot(a[0], b[1]) + dot(a[1], b[0]))


def join(parts, axis):
    return parts[0] if len(parts) == 1 else jnp.concatenate(parts, axis=axis)


def sum_dots(parts, mat, dims_width):
    if dims_width % 128 == 0:
        a = (join([p[0] for p in parts], 1), join([p[1] for p in parts], 1))
        return dot3(a, (mat[0][...], mat[1][...]), NN)
    total = None
    for e, p in enumerate(parts):
        rows = pl.ds(e * dims_width, dims_width)
        term = dot3(p, (mat[0][rows, :], mat[1][rows, :]), NN)
        total = term if total is None else total + term
    return total


def pairwise(a, v, i):
    ny = v.shape[2]
    if ny % 128:
        return [(c, dot3(a, split(v[c]), NN)) for c in (2 * i, 2 * i + 1)]
    t = dot3(a, split(join([v[2 * i], v[2 * i + 1]], 1)), NN)
    return [(2 * i, t[:, :ny]), (2 * i + 1, t[:, ny:])]


def whole(shape):
    return pl.BlockSpec(shape, lambda *_: (0,) * len(shape))


def forward_z(residual, basis_zt, where, chunks, peers, part):
    nx, ny, nz = residual.shape
    xb = 8
    group = peers * part

    def kernel(where_ref, r_ref, b_ref, *outs):
        me = where_ref[0]
        rows = [
            b_ref[pl.ds(pl.multiple_of(k * group + (me ^ d) * part, part), part), :]
            for k in chunks
            for d in range(peers)
        ]
        basis = split(join(rows, 0))

        @pl.loop(0, xb // 4)
        def _(step):
            for x in (4 * step + u for u in range(4)):
                t = dot3(basis, split(r_ref[x]), NT)
                for n, out in enumerate(outs):
                    out[x] = t[n * part : (n + 1) * part, :]

    count = len(chunks) * peers
    outs = pl.pallas_call(
        kernel,
        grid_spec=pltpu.PrefetchScalarGridSpec(
            num_scalar_prefetch=1,
            grid=(nx // xb,),
            in_specs=[
                pl.BlockSpec((xb, ny, nz), lambda i, w: (i, 0, 0)),
                pl.BlockSpec(basis_zt.shape, lambda i, w: (0, 0)),
            ],
            out_specs=[pl.BlockSpec((xb, part, ny), lambda i, w: (i, 0, 0))] * count,
        ),
        out_shape=[jax.ShapeDtypeStruct((nx, part, ny), F32)] * count,
        compiler_params=params(1),
        cost_estimate=cost(6 * nx * ny * nz * len(chunks) * group, nx * ny * nz * 4),
        name="forward_z",
    )(where, residual, basis_zt)
    return [outs[n * peers : (n + 1) * peers] for n in range(len(chunks))]


def forward_x(pieces, bxt, peers, after):
    nx, part, ny = pieces[0].shape
    full = nx * len(pieces)
    wide = full // peers

    def kernel(_, bh, bl, *refs):
        ins, outs, v = refs[: len(pieces)], refs[len(pieces) : -1], refs[-1]
        for c in range(part):
            for d, r in enumerate(ins):
                v[c, d * nx : (d + 1) * nx, :] = r[:, c, :]

        @pl.loop(0, part // 2)
        def _(i):
            for c, t in pairwise((bh[...], bl[...]), v, i):
                for e, out in enumerate(outs):
                    out[c] = t[e * wide : (e + 1) * wide, :]

    return pl.pallas_call(
        kernel,
        out_shape=[jax.ShapeDtypeStruct((part, wide, ny), F32)] * peers,
        in_specs=[pl.BlockSpec(memory_space=pl.ANY)]
        + [pl.BlockSpec(memory_space=pltpu.VMEM)] * (2 + len(pieces)),
        out_specs=[pl.BlockSpec(memory_space=pltpu.VMEM)] * peers,
        compiler_params=params(0),
        cost_estimate=cost(6 * full * full * part * ny, 8 * full * part * ny),
        scratch_shapes=[pltpu.VMEM((part, full, ny), F32)],
        name="forward_x",
    )(after, *bxt, *pieces)


def middle_y(pieces, by, byt, shift, eigen_y, after):
    part, wide, ny = pieces[0].shape
    peers = len(pieces)
    full = peers * ny
    cb = 2 if part % 2 == 0 and wide % 8 == 0 else 1

    def kernel(_, bh, bl, th, tl, shift_ref, ey_ref, *refs):
        ins, outs = refs[:peers], refs[peers:]
        parts = [split(r[...].reshape(cb * wide, ny)) for r in ins]
        spectrum = sum_dots(parts, (bh, bl), ny)
        ey = ey_ref[...]
        scaled = [
            spectrum[n * wide : (n + 1) * wide, :] / (shift_ref[n] + ey)
            for n in range(cb)
        ]
        back = dot3(split(join(scaled, 0)), (th[...], tl[...]), NN)
        for e, out in enumerate(outs):
            out[...] = back[:, e * ny : (e + 1) * ny].reshape(cb, wide, ny)

    spec = pl.BlockSpec((cb, wide, ny), lambda i: (i, 0, 0))
    return pl.pallas_call(
        kernel,
        grid=(part // cb,),
        out_shape=[jax.ShapeDtypeStruct((part, wide, ny), F32)] * peers,
        in_specs=[pl.BlockSpec(memory_space=pl.ANY)]
        + [whole((full, full))] * 4
        + [pl.BlockSpec((cb, wide, 1), lambda i: (i, 0, 0)), whole((1, full))]
        + [spec] * peers,
        out_specs=[spec] * peers,
        compiler_params=params(1),
        cost_estimate=cost(12 * full * full * part * wide, 8 * full * part * wide),
        name="middle_y",
    )(after, *by, *byt, shift, eigen_y, *pieces)


def backward_x(pieces, bx, peers, after, cuts=1):
    part, wide, ny = pieces[0].shape
    full = wide * len(pieces)
    nx = full // peers // cuts

    def kernel(_, bh, bl, *refs):
        ins, outs, v, w = refs[: len(pieces)], refs[len(pieces) : -2], refs[-2], refs[-1]
        for n, r in enumerate(ins):
            v[:, n * wide : (n + 1) * wide, :] = r[...]

        @pl.loop(0, part // 2)
        def _(i):
            for c, t in pairwise((bh[...], bl[...]), v, i):
                w[c] = t

        for c in range(part):
            for n, out in enumerate(outs):
                at = (n % peers) * cuts + n // peers
                out[:, c, :] = w[c, at * nx : (at + 1) * nx, :]

    return pl.pallas_call(
        kernel,
        out_shape=[jax.ShapeDtypeStruct((nx, part, ny), F32)] * (peers * cuts),
        in_specs=[pl.BlockSpec(memory_space=pl.ANY)]
        + [pl.BlockSpec(memory_space=pltpu.VMEM)] * (2 + len(pieces)),
        out_specs=[pl.BlockSpec(memory_space=pltpu.VMEM)] * (peers * cuts),
        compiler_params=params(0),
        cost_estimate=cost(6 * full * full * part * ny, 8 * full * part * ny),
        scratch_shapes=[pltpu.VMEM((part, full, ny), F32)] * 2,
        name="backward_x",
    )(after, *bx, *pieces)


def backward_z(pieces, basis_zt, where, adjoint, coefficient, cut=0, cuts=1, before=()):
    nx, ny, nz = adjoint.shape
    peers, part = len(pieces[0]), pieces[0][0].shape[1]
    group = peers * part
    chunks = len(pieces)
    xb = 8
    steps = nx // xb // cuts
    flat = [p for chunk in pieces for p in chunk]
    last = cut == cuts - 1

    def kernel(where_ref, b_ref, adj_ref, coef_ref, *refs):
        if before:
            low_ref, refs = refs[4], refs[6:]
        ins, outs = refs[: len(flat)], refs[len(flat) :]
        next_ref, w_ref = outs[:2]
        edges, slabs = outs[2:4], outs[4:]
        me, i = where_ref[0], pl.program_id(0)
        rows = [
            b_ref[pl.ds(pl.multiple_of(k * group + (me ^ d) * part, part), part), :]
            for k in range(chunks)
            for d in range(peers)
        ]
        basis = split(join(rows, 0))

        @pl.loop(0, xb // 4)
        def _(step):
            for x in (4 * step + u for u in range(4)):
                v = split(join([r[x] for r in ins], 0))
                correction = dot3(v, basis, TN)
                next_ref[x] = adj_ref[x] + correction
                w_ref[x] = coef_ref[x].astype(F32) * correction

        for n in range(2):

            @pl.when(where_ref[1] % 2 == n)
            def _():
                for j in range(3):
                    edges[n][j] = w_ref[:, ny - 3 + j, :]
                    edges[1 - n][j] = w_ref[:, j, :]

            if last:

                @pl.when((i == 0) & (me % 2 == n))
                def _():
                    slabs[1 - n][...] = low_ref[...] if before else w_ref[:3]

                @pl.when((i == steps - 1) & (me % 2 == n))
                def _():
                    slabs[n][...] = w_ref[xb - 3 :]

        if not last:

            @pl.when(i == 0)
            def _():
                slabs[0][...] = w_ref[:3]

    skip = cut * steps
    field = pl.BlockSpec((xb, ny, nz), lambda i, w: (i + skip, 0, 0))
    slab = pl.BlockSpec((3, ny, nz), lambda i, w: (0, 0, 0))
    edge = pl.BlockSpec((3, xb, nz), lambda i, w: (0, i + skip, 0))
    whole_piece = pl.BlockSpec((xb, part, ny), lambda i, w: (i + skip, 0, 0))
    cut_piece = pl.BlockSpec((xb, part, ny), lambda i, w: (i, 0, 0))
    anywhere = pl.BlockSpec(memory_space=pl.ANY)
    count = 2 if last else 1
    shapes = [(nx, ny, nz)] * 2 + [(3, nx, nz)] * 2 + [(3, ny, nz)] * count
    return pl.pallas_call(
        kernel,
        grid_spec=pltpu.PrefetchScalarGridSpec(
            num_scalar_prefetch=1,
            grid=(steps,),
            in_specs=[pl.BlockSpec(basis_zt.shape, lambda i, w: (0, 0)), field, field]
            + ([anywhere] * 4 + [slab, anywhere] if before else [])
            + [whole_piece if p.shape[0] == nx else cut_piece for p in flat],
            out_specs=[field] * 2 + [edge] * 2 + [slab] * count,
        ),
        out_shape=[jax.ShapeDtypeStruct(shape, F32) for shape in shapes],
        input_output_aliases={4 + n: n for n in range(4)} if before else {},
        compiler_params=params(1),
        cost_estimate=cost(6 * nx * ny * nz * nz // cuts, 22 * nx * ny * nz // cuts),
        name="backward_z",
    )(where, basis_zt, adjoint, coefficient, *before, *flat)


def band(n):
    out = np.zeros((2 * n, n), np.float32)
    for j in range(-3, 4):
        out[:n] += MASS[j + 3] * np.eye(n, k=j, dtype=np.float32)
        out[n:] += STIFF[j + 3] * np.eye(n, k=j, dtype=np.float32)
    return out


def taps(load, mass=True, stiff=True):
    mid = load(0)
    pair = [load(j) + load(-j) for j in (1, 2, 3)]
    out = []
    for use, co in ((mass, MASS), (stiff, STIFF)):
        if use:
            out.append(co[3] * mid + co[4] * pair[0] + co[5] * pair[1] + co[6] * pair[2])
    return out


def stencil(weighted, residual, bands, first=1, count=0, halos=None, after=None):
    nx, ny, nz = weighted.shape
    xb, unroll = 8, 4
    steps = nx // xb
    halves = nz // 128
    outer = halos is not None
    rows = lax.axis_size("row")

    def kernel(_, bh, bl, *refs):
        i = pl.program_id(0)
        if outer:
            where_ref, xa, xc, prev, cur, nxt, r_ref, out, win, ps, qs = refs
        else:
            prev, cur, nxt, r_ref, out, win, ps, qs = refs

        @pl.when(i == 0)
        def _():
            zero = jnp.zeros((unroll, halves, 8, 128), F32)
            for ref in (ps, qs):
                ref[:, :, :8, :] = zero
                ref[:, :, 8 + ny :, :] = zero

        win[:3] = prev[xb - 3 :]
        win[3 : 3 + xb] = cur[...]
        win[3 + xb :] = nxt[:3]
        if outer:
            me = where_ref[0]

            @pl.when(i == 0)
            def _():
                low = jnp.where(me % 2 == 0, xc[...], xa[...])
                win[:3] = jnp.where(me == 0, 0.0, low)

            @pl.when(i == 1)
            def _():
                high = jnp.where(me % 2 == 0, xa[...], xc[...])
                win[3 + xb :] = jnp.where(me == rows - 1, 0.0, high)

        @pl.loop(0, xb // unroll)
        def _(step):
            for u in range(unroll):
                x = step * unroll + u
                p, q = taps(lambda o: win[x + 3 + o])
                for h in range(halves):
                    cols = slice(h * 128, (h + 1) * 128)
                    ps[u, h, 8 : 8 + ny, :] = p[:, cols]
                    qs[u, h, 8 : 8 + ny, :] = q[:, cols]
                first_terms, second_terms = [], []
                for h in range(halves):
                    mp, kp = taps(lambda o: ps[u, h, 8 + o : 8 + o + ny, :])
                    (mq,) = taps(lambda o: qs[u, h, 8 + o : 8 + o + ny, :], stiff=False)
                    first_terms.append(kp + mq)
                    second_terms.append(mp)
                both = split(join(first_terms + second_terms, 1))
                out[x] = r_ref[x] - dot3(both, (bh[...], bl[...]), NN)

    if outer:
        at = lambda i: i * (steps - 1)
        count = 2
    else:
        at = lambda i: i + first

    def block(shift):
        return pl.BlockSpec(
            (xb, ny, nz),
            lambda i: (jnp.clip(at(i) + shift, 0, steps - 1), 0, 0),
        )

    extra = list(halos) if outer else []
    return pl.pallas_call(
        kernel,
        grid=(count,),
        in_specs=[pl.BlockSpec(memory_space=pl.ANY)]
        + [whole(b.shape) for b in bands]
        + ([pl.BlockSpec(memory_space=pltpu.SMEM)] if outer else [])
        + [whole(e.shape) for e in extra[1:]]
        + [block(-1), block(0), block(1), block(0)],
        out_specs=block(0),
        out_shape=jax.ShapeDtypeStruct((nx, ny, nz), F32),
        scratch_shapes=[pltpu.VMEM((xb + 6, ny, nz), F32)]
        + [pltpu.VMEM((unroll, halves, ny + 16, 128), F32)] * 2,
        input_output_aliases={} if after is None else {0: 0},
        compiler_params=params(1),
        cost_estimate=cost(12 * count * xb * ny * nz * nz, 12 * count * xb * ny * nz),
        name="stencil_outer" if outer else "stencil_inner",
    )(weighted if after is None else after, *bands, *extra, weighted, weighted, weighted, residual)


def stencil_sides(partial, where, bands, edges, corners):
    nx, ny, nz = partial.shape

    rows, cols = lax.axis_size("row"), lax.axis_size("col")

    def kernel(where_ref, bh, bl, ea, ec, ca, cc, r_ref, out, ext, ph, qh):
        me, mine = where_ref[0], where_ref[1]
        for side in range(2):

            @pl.when(pl.program_id(0) == side)
            def _():
                ph[...] = jnp.zeros_like(ph)
                qh[...] = jnp.zeros_like(qh)
                base = 5 if side == 0 else 16
                near = mine % 2 == 1 - side
                pick = jnp.where(near, 0, 1)
                border = mine == (0 if side == 0 else cols - 1)
                for j in range(3):
                    edge = jnp.where(near, ea[j], ec[j])
                    even = me % 2 == 0
                    low = jnp.where(even, cc[pick, j], ca[pick, j])
                    high = jnp.where(even, ca[pick, j], cc[pick, j])
                    ext[:8] = jnp.where(border | (me == 0), 0.0, low)
                    ext[8 : 8 + nx] = jnp.where(border, 0.0, edge)
                    ext[8 + nx :] = jnp.where(border | (me == rows - 1), 0.0, high)
                    p, q = taps(lambda o: ext[8 + o : 8 + o + nx, :])
                    ph[:, base + j, :] = p
                    qh[:, base + j, :] = q

        mp, kp = taps(lambda o: ph[:, 8 + o : 16 + o, :])
        (mq,) = taps(lambda o: qh[:, 8 + o : 16 + o, :], stiff=False)
        both = split(jnp.concatenate([kp + mq, mp], 2).reshape(nx * 8, 2 * nz))
        image = dot3(both, (bh[...], bl[...]), NN)
        out[...] = r_ref[...] - image.reshape(nx, 8, nz)

    field = pl.BlockSpec((nx, 8, nz), lambda i: (0, i * (ny // 8 - 1), 0))
    return pl.pallas_call(
        kernel,
        grid=(2,),
        in_specs=[pl.BlockSpec(memory_space=pltpu.SMEM)]
        + [whole(b.shape) for b in bands]
        + [whole(e.shape) for e in edges]
        + [whole(c.shape) for c in corners]
        + [field],
        out_specs=field,
        out_shape=jax.ShapeDtypeStruct((nx, ny, nz), F32),
        scratch_shapes=[pltpu.VMEM((nx + 16, nz), F32)]
        + [pltpu.VMEM((nx, 24, nz), F32)] * 2,
        input_output_aliases={7: 0},
        compiler_params=params(1),
        cost_estimate=cost(12 * nx * 16 * nz * nz, 128 * nx * nz),
        name="stencil_sides",
    )(where, *bands, *edges, *corners, partial)


def exchange(pieces, axis):
    n = len(pieces)
    out = [pieces[0]] + [None] * (n - 1)
    for d in range(n - 1, 0, -1):
        out[d] = lax.ppermute(pieces[d], axis, [(i, i ^ d) for i in range(n)])
    return out


def swap(array, axis, near):
    n = lax.axis_size(axis)
    other = [i ^ 1 if near else (i + 1 if i % 2 else i - 1) for i in range(n)]
    return lax.ppermute(
        array, axis, [(i, j if 0 <= j < n else i) for i, j in enumerate(other)]
    )


def schedule(chunks):
    order = [("z", 0), ("z", 1)][:chunks]
    if chunks == 4:
        order += [("x", 0), ("y", 0), ("x", 1), ("b", 0), ("y", 1), ("x", 2)]
        order += [("b", 1), ("y", 2), ("x", 3), ("b", 2), ("y", 3), ("b", 3)]
    else:
        order += [(s, k) for k in range(chunks) for s in ("x", "y", "b")]
    return order


def cut_count(nx):
    return 2 if nx % 16 == 0 and nx // 8 >= 6 else 1


def chunk_count(nz, rows):
    return max(1, min(4, nz // (rows * 8)))


def shards(residual, adjoint, coefficient, basis_x, basis_y, basis_z, eigen_x, eigen_y, eigen_z):
    nx, ny, nz = residual.shape
    rows, cols = lax.axis_size("row"), lax.axis_size("col")
    ri, ci = lax.axis_index("row"), lax.axis_index("col")
    width_x = nx * rows
    wide = width_x // cols
    chunks = chunk_count(nz, rows)
    part = nz // (rows * chunks)
    where = jnp.stack([ri, ci]).astype(jnp.int32)
    steps = nx // 8
    cuts = cut_count(nx)

    basis_zt = basis_z.T
    bx = jnp.concatenate(
        [lax.dynamic_slice_in_dim(basis_x, (ri ^ d) * nx, nx, 0) for d in range(rows)], 0
    )
    bx = jnp.concatenate(
        [lax.dynamic_slice_in_dim(bx, (ci ^ e) * wide, wide, 1) for e in range(cols)], 1
    )
    by = jnp.concatenate(
        [lax.dynamic_slice_in_dim(basis_y, (ci ^ e) * ny, ny, 0) for e in range(cols)], 0
    )
    bx2, by2 = split_outside(bx), split_outside(by)
    bxt2, byt2 = tuple(b.T for b in bx2), tuple(b.T for b in by2)
    ex = lax.dynamic_slice_in_dim(eigen_x, ci * wide, wide)
    ez = lax.dynamic_slice_in_dim(eigen_z.reshape(chunks, rows, part), ri, 1, 1)[:, 0]
    shift = (ez[:, :, None] + ex[None, None, :])[..., None]
    ey = eigen_y[None, :]
    bands = split_outside(jnp.asarray(band(nz)))

    fw, mid, ret, back = ([None] * chunks for _ in range(4))
    last = where
    for stage, k in schedule(chunks):
        if stage == "z":
            these = (k,) if k == 0 else tuple(range(k, chunks))
            outs = forward_z(residual, basis_zt, where, these, rows, part)
            for n, out in zip(these, outs):
                fw[n] = (out, "row")
            last = outs[-1][0]
        elif stage == "x":
            out = forward_x(fw[k], bxt2, cols, last)
        elif stage == "y":
            out = middle_y(mid[k], by2, byt2, shift[k], ey, last)
        else:
            parts = cuts if k == chunks - 1 else 1
            out = backward_x(ret[k], bx2, rows, last, parts)
        if stage == "z":
            fw[k] = exchange(*fw[k])
        elif stage == "x":
            mid[k] = exchange(out, "col")
        elif stage == "y":
            ret[k] = exchange(out, "col")
        else:
            back[k] = exchange(out[:rows], "row")
        if stage == "x" and k + 2 < chunks:
            fw[k + 2] = exchange(*fw[k + 2])
        if stage != "z":
            last = out[0]
    late = exchange(out[rows:], "row") if cuts > 1 else None
    fields = (basis_zt, where, adjoint, coefficient)
    if cuts > 1:
        early = backward_z(back, *fields, 0, cuts)
        begun = stencil(early[1], residual, bands, 1, steps // 2 - 2)
        back = back[:-1] + [late]
        done = backward_z(back, *fields, 1, cuts, (*early, begun))
        rest = (steps // 2 - 1, steps // 2)
    else:
        done = backward_z(back, *fields)
        begun, rest = None, (1, steps - 2)
    adjoint_next, weighted, ea, ec, xa, xc = done
    ea, ec = swap(ea, "col", True), swap(ec, "col", False)
    xa, xc = swap(xa, "row", True), swap(xc, "row", False)
    inner = stencil(weighted, residual, bands, *rest, after=begun)
    sides, _ = lax.optimization_barrier((jnp.stack([ea, ec]), inner))
    low, high = sides[:, :, :8], sides[:, :, -8:]
    even = ri % 2 == 0
    ca = swap(jnp.where(even, high, low), "row", True)
    cc = swap(jnp.where(even, low, high), "row", False)
    outer = stencil(weighted, residual, bands, halos=(where, xa, xc), after=inner)
    residual_next = stencil_sides(outer, where, bands, (ea, ec), (ca, cc))
    return adjoint_next, residual_next


def solution(mesh):
    field = P("row", "col", None)
    return jax.shard_map(
        shards,
        mesh=mesh,
        in_specs=(field,) * 3 + (P(),) * 6,
        out_specs=(field, field),
        check_vma=False,
    )
```

```python
import jax
import jax.numpy as jnp
from jax import lax
from jax.experimental import pallas as pl
from jax.experimental.pallas import tpu as pltpu
from jax.sharding import PartitionSpec as P


MASS = tuple(t / 5040 for t in (1.0, 120.0, 1191.0, 2416.0, 1191.0, 120.0, 1.0))
STIFF = (-1.0 / 120, -0.2, -0.125, 2.0 / 3.0, -0.125, -0.2, -1.0 / 120)
F32, BF16 = jnp.float32, jnp.bfloat16
NN = (((1,), (0,)), ((), ()))
NT = (((1,), (1,)), ((), ()))


def params(n, limit=56 << 20):
    return pltpu.CompilerParams(
        dimension_semantics=("arbitrary",) * n, vmem_limit_bytes=limit
    )


def cost(flops, nbytes):
    return pl.CostEstimate(flops=flops, bytes_accessed=nbytes, transcendentals=0)


def split(v):
    high = v.astype(BF16)
    return high, (v - high.astype(F32)).astype(BF16)


def split_outside(v):
    high = lax.reduce_precision(v, 8, 7)
    return high.astype(BF16), (v - high).astype(BF16)


def dot3(a, b, dims):
    def dot(p, q):
        return lax.dot_general(p, q, dims, preferred_element_type=F32)

    return dot(a[0], b[0]) + (dot(a[0], b[1]) + dot(a[1], b[0]))


def join(parts, axis):
    return parts[0] if len(parts) == 1 else jnp.concatenate(parts, axis=axis)


def sum_dots(parts, mat, dims_width):
    if dims_width % 128 == 0:
        a = (join([p[0] for p in parts], 1), join([p[1] for p in parts], 1))
        return dot3(a, (mat[0][...], mat[1][...]), NN)
    total = None
    for e, p in enumerate(parts):
        rows = pl.ds(e * dims_width, dims_width)
        term = dot3(p, (mat[0][rows, :], mat[1][rows, :]), NN)
        total = term if total is None else total + term
    return total


def products(mat, v, w):
    full, ny = v.shape[1:]
    rows = full // 2

    @pl.loop(0, v.shape[0])
    def _(i):
        at = pl.ds(pl.multiple_of((i % 2) * rows, rows), rows)
        a = (mat[0][at, :], mat[1][at, :])
        c = 2 * (i // 2)
        if ny % 128:
            w[c, at, :] = dot3(a, split(v[c]), NN)
            w[c + 1, at, :] = dot3(a, split(v[c + 1]), NN)
        else:
            t = dot3(a, split(join([v[c], v[c + 1]], 1)), NN)
            w[c, at, :] = t[:, :ny]
            w[c + 1, at, :] = t[:, ny:]


def whole(shape):
    return pl.BlockSpec(shape, lambda *_: (0,) * len(shape))


def forward_z(residual, basis_zt, where, chunks, peers, part):
    nx, ny, nz = residual.shape
    xb = 32 if nx % 32 == 0 else 8
    group = peers * part

    def kernel(where_ref, r_ref, b_ref, *outs):
        me = where_ref[0]
        rows = [
            b_ref[pl.ds(pl.multiple_of(k * group + (me ^ d) * part, part), part), :]
            for k in chunks
            for d in range(peers)
        ]
        width = len(rows) * part
        both = jnp.concatenate(split(join(rows, 0)), 0)

        @pl.loop(0, xb // 4)
        def _(step):
            high, low = split(r_ref[pl.ds(4 * step, 4)].reshape(4 * ny, nz))
            product = lax.dot_general(high, both, NT, preferred_element_type=F32)
            product += lax.dot_general(low, both, NT, preferred_element_type=F32)
            for u in range(4):
                t = product[u * ny : (u + 1) * ny, :].T
                t = t[:width] + t[width:]
                for n, out in enumerate(outs):
                    out[4 * step + u] = t[n * part : (n + 1) * part, :]

    count = len(chunks) * peers
    outs = pl.pallas_call(
        kernel,
        grid_spec=pltpu.PrefetchScalarGridSpec(
            num_scalar_prefetch=1,
            grid=(nx // xb,),
            in_specs=[
                pl.BlockSpec((xb, ny, nz), lambda i, w: (i, 0, 0)),
                pl.BlockSpec(basis_zt.shape, lambda i, w: (0, 0)),
            ],
            out_specs=[pl.BlockSpec((xb, part, ny), lambda i, w: (i, 0, 0))] * count,
        ),
        out_shape=[jax.ShapeDtypeStruct((nx, part, ny), F32)] * count,
        compiler_params=params(1),
        cost_estimate=cost(6 * nx * ny * nz * len(chunks) * group, nx * ny * nz * 4),
        name="forward_z",
    )(where, residual, basis_zt)
    return [outs[n * peers : (n + 1) * peers] for n in range(len(chunks))]


def forward_x(pieces, bxt, peers, after):
    nx, part, ny = pieces[0].shape
    full = nx * len(pieces)
    wide = full // peers

    def kernel(_, bh, bl, *refs):
        ins, outs, v, w = refs[: len(pieces)], refs[len(pieces) : -2], refs[-2], refs[-1]
        for c in range(part):
            for d, r in enumerate(ins):
                v[c, d * nx : (d + 1) * nx, :] = r[:, c, :]

        products((bh, bl), v, w)
        for e, out in enumerate(outs):
            out[...] = w[:, e * wide : (e + 1) * wide, :]

    return pl.pallas_call(
        kernel,
        out_shape=[jax.ShapeDtypeStruct((part, wide, ny), F32)] * peers,
        in_specs=[pl.BlockSpec(memory_space=pl.ANY)]
        + [pl.BlockSpec(memory_space=pltpu.VMEM)] * (2 + len(pieces)),
        out_specs=[pl.BlockSpec(memory_space=pltpu.VMEM)] * peers,
        compiler_params=params(0),
        cost_estimate=cost(6 * full * full * part * ny, 8 * full * part * ny),
        scratch_shapes=[pltpu.VMEM((part, full, ny), F32)] * 2,
        name="forward_x",
    )(after, *bxt, *pieces)


def middle_y(pieces, by, byt, shift, eigen_y, after):
    part, wide, ny = pieces[0].shape
    peers = len(pieces)
    full = peers * ny
    cb = 2 if part % 2 == 0 and wide % 8 == 0 else 1

    def kernel(_, bh, bl, th, tl, shift_ref, ey_ref, *refs):
        ins, outs = refs[:peers], refs[peers:]
        parts = [split(r[...].reshape(cb * wide, ny)) for r in ins]
        spectrum = sum_dots(parts, (bh, bl), ny)
        ey = ey_ref[...]
        scaled = [
            spectrum[n * wide : (n + 1) * wide, :] / (shift_ref[n] + ey)
            for n in range(cb)
        ]
        back = dot3(split(join(scaled, 0)), (th[...], tl[...]), NN)
        for e, out in enumerate(outs):
            out[...] = back[:, e * ny : (e + 1) * ny].reshape(cb, wide, ny)

    spec = pl.BlockSpec((cb, wide, ny), lambda i: (i, 0, 0))
    return pl.pallas_call(
        kernel,
        grid=(part // cb,),
        out_shape=[jax.ShapeDtypeStruct((part, wide, ny), F32)] * peers,
        in_specs=[pl.BlockSpec(memory_space=pl.ANY)]
        + [whole((full, full))] * 4
        + [pl.BlockSpec((cb, wide, 1), lambda i: (i, 0, 0)), whole((1, full))]
        + [spec] * peers,
        out_specs=[spec] * peers,
        compiler_params=params(1),
        cost_estimate=cost(12 * full * full * part * wide, 8 * full * part * wide),
        name="middle_y",
    )(after, *by, *byt, shift, eigen_y, *pieces)


def backward_x(pieces, bx, peers, after, cuts=1):
    part, wide, ny = pieces[0].shape
    full = wide * len(pieces)
    nx = full // peers // cuts

    def kernel(_, bh, bl, *refs):
        ins, outs, v, w = refs[: len(pieces)], refs[len(pieces) : -2], refs[-2], refs[-1]
        for n, r in enumerate(ins):
            v[:, n * wide : (n + 1) * wide, :] = r[...]

        products((bh, bl), v, w)
        for c in range(part):
            for n, out in enumerate(outs):
                at = (n % peers) * cuts + n // peers
                out[:, c, :] = w[c, at * nx : (at + 1) * nx, :]

    return pl.pallas_call(
        kernel,
        out_shape=[jax.ShapeDtypeStruct((nx, part, ny), F32)] * (peers * cuts),
        in_specs=[pl.BlockSpec(memory_space=pl.ANY)]
        + [pl.BlockSpec(memory_space=pltpu.VMEM)] * (2 + len(pieces)),
        out_specs=[pl.BlockSpec(memory_space=pltpu.VMEM)] * (peers * cuts),
        compiler_params=params(0),
        cost_estimate=cost(6 * full * full * part * ny, 8 * full * part * ny),
        scratch_shapes=[pltpu.VMEM((part, full, ny), F32)] * 2,
        name="backward_x",
    )(after, *bx, *pieces)


def backward_z(pieces, basis_zt, where, adjoint, coefficient, cut=0, cuts=1, before=()):
    nx, ny, nz = adjoint.shape
    peers, part = len(pieces[0]), pieces[0][0].shape[1]
    group = peers * part
    chunks = len(pieces)
    xb = 16 if nx // cuts % 16 == 0 else 8
    steps = nx // xb // cuts
    flat = [p for chunk in pieces for p in chunk]
    last = cut == cuts - 1

    def kernel(where_ref, b_ref, adj_ref, coef_ref, *refs):
        if before:
            low_ref, refs = refs[4], refs[6:]
        ins, outs = refs[: len(flat)], refs[len(flat) :]
        next_ref, w_ref = outs[:2]
        edges, slabs = outs[2:4], outs[4:]
        me, i = where_ref[0], pl.program_id(0)
        rows = [
            b_ref[pl.ds(pl.multiple_of(k * group + (me ^ d) * part, part), part), :]
            for k in range(chunks)
            for d in range(peers)
        ]
        basis = split(join(rows, 0))

        @pl.loop(0, xb // 4)
        def _(step):
            planes = pl.ds(4 * step, 4)
            v = [join([r[4 * step + u] for r in ins], 0).T for u in range(4)]
            correction = dot3(split(join(v, 0)), basis, NN).reshape(4, ny, nz)
            next_ref[planes] = adj_ref[planes] + correction
            w_ref[planes] = coef_ref[planes].astype(F32) * correction

        for n in range(2):

            @pl.when(where_ref[1] % 2 == n)
            def _():
                for j in range(3):
                    edges[n][j] = w_ref[:, ny - 3 + j, :]
                    edges[1 - n][j] = w_ref[:, j, :]

            if last:

                @pl.when((i == 0) & (me % 2 == n))
                def _():
                    slabs[1 - n][...] = low_ref[...] if before else w_ref[:3]

                @pl.when((i == steps - 1) & (me % 2 == n))
                def _():
                    slabs[n][...] = w_ref[xb - 3 :]

        if not last:

            @pl.when(i == 0)
            def _():
                slabs[0][...] = w_ref[:3]

    skip = cut * steps
    field = pl.BlockSpec((xb, ny, nz), lambda i, w: (i + skip, 0, 0))
    slab = pl.BlockSpec((3, ny, nz), lambda i, w: (0, 0, 0))
    edge = pl.BlockSpec((3, xb, nz), lambda i, w: (0, i + skip, 0))
    whole_piece = pl.BlockSpec((xb, part, ny), lambda i, w: (i + skip, 0, 0))
    cut_piece = pl.BlockSpec((xb, part, ny), lambda i, w: (i, 0, 0))
    anywhere = pl.BlockSpec(memory_space=pl.ANY)
    count = 2 if last else 1
    shapes = [(nx, ny, nz)] * 2 + [(3, nx, nz)] * 2 + [(3, ny, nz)] * count
    return pl.pallas_call(
        kernel,
        grid_spec=pltpu.PrefetchScalarGridSpec(
            num_scalar_prefetch=1,
            grid=(steps,),
            in_specs=[pl.BlockSpec(basis_zt.shape, lambda i, w: (0, 0)), field, field]
            + ([anywhere] * 4 + [slab, anywhere] if before else [])
            + [whole_piece if p.shape[0] == nx else cut_piece for p in flat],
            out_specs=[field] * 2 + [edge] * 2 + [slab] * count,
        ),
        out_shape=[jax.ShapeDtypeStruct(shape, F32) for shape in shapes],
        input_output_aliases={4 + n: n for n in range(4)} if before else {},
        compiler_params=params(1),
        cost_estimate=cost(6 * nx * ny * nz * nz // cuts, 22 * nx * ny * nz // cuts),
        name="backward_z",
    )(where, basis_zt, adjoint, coefficient, *before, *flat)


def band(n):
    row = lax.broadcasted_iota(jnp.int32, (2 * n, n), 0)
    offset = lax.broadcasted_iota(jnp.int32, (2 * n, n), 1) - row % n
    out = jnp.zeros((2 * n, n), F32)
    for j in range(-3, 4):
        out = jnp.where(offset == j, jnp.where(row < n, MASS[j + 3], STIFF[j + 3]), out)
    return out


def taps(load, mass=True, stiff=True):
    mid = load(0)
    pair = [load(j) + load(-j) for j in (1, 2, 3)]
    out = []
    for use, co in ((mass, MASS), (stiff, STIFF)):
        if use:
            out.append(co[3] * mid + co[4] * pair[0] + co[5] * pair[1] + co[6] * pair[2])
    return out


def stencil(weighted, residual, bands, first=1, count=0, halos=None, after=None):
    nx, ny, nz = weighted.shape
    xb, unroll = 8, 4 if halos is None else 2
    steps = nx // xb
    halves = nz // 128
    outer = halos is not None
    rows = lax.axis_size("row")

    def kernel(_, bh, bl, *refs):
        i = pl.program_id(0)
        if outer:
            where_ref, xa, xc, prev, cur, nxt, r_ref, out, win, ps, qs, high, low = refs
        else:
            prev, cur, nxt, r_ref, out, win, ps, qs, high, low = refs

        @pl.when(i == 0)
        def _():
            zero = jnp.zeros((unroll, halves, 8, 128), F32)
            for ref in (ps, qs):
                ref[:, :, :8, :] = zero
                ref[:, :, 8 + ny :, :] = zero

        win[:3] = prev[xb - 3 :]
        win[3 : 3 + xb] = cur[...]
        win[3 + xb :] = nxt[:3]
        if outer:
            me = where_ref[0]

            @pl.when(i == 0)
            def _():
                low = jnp.where(me % 2 == 0, xc[...], xa[...])
                win[:3] = jnp.where(me == 0, 0.0, low)

            @pl.when(i == 1)
            def _():
                high = jnp.where(me % 2 == 0, xa[...], xc[...])
                win[3 + xb :] = jnp.where(me == rows - 1, 0.0, high)

        @pl.loop(0, xb // unroll)
        def _(step):
            for u in range(unroll):
                x = step * unroll + u
                p, q = taps(lambda o: win[x + 3 + o])
                for h in range(halves):
                    cols = slice(h * 128, (h + 1) * 128)
                    ps[u, h, 8 : 8 + ny, :] = p[:, cols]
                    qs[u, h, 8 : 8 + ny, :] = q[:, cols]
                first_terms, second_terms = [], []
                for h in range(halves):
                    mp, kp = taps(lambda o: ps[u, h, 8 + o : 8 + o + ny, :])
                    (mq,) = taps(lambda o: qs[u, h, 8 + o : 8 + o + ny, :], stiff=False)
                    first_terms.append(kp + mq)
                    second_terms.append(mp)
                rows_u = slice(u * ny, (u + 1) * ny)
                both = split(join(first_terms + second_terms, 1))
                high[rows_u], low[rows_u] = both
            planes = pl.ds(step * unroll, unroll)
            image = dot3((high[...], low[...]), (bh[...], bl[...]), NN)
            out[planes] = r_ref[planes] - image.reshape(unroll, ny, nz)

    if outer:
        at = lambda i: i * (steps - 1)
        count = 2
    else:
        at = lambda i: i + first

    def block(shift):
        return pl.BlockSpec(
            (xb, ny, nz),
            lambda i: (jnp.clip(at(i) + shift, 0, steps - 1), 0, 0),
        )

    extra = list(halos) if outer else []
    return pl.pallas_call(
        kernel,
        grid=(count,),
        in_specs=[pl.BlockSpec(memory_space=pl.ANY)]
        + [whole(b.shape) for b in bands]
        + ([pl.BlockSpec(memory_space=pltpu.SMEM)] if outer else [])
        + [whole(e.shape) for e in extra[1:]]
        + [block(-1), block(0), block(1), block(0)],
        out_specs=block(0),
        out_shape=jax.ShapeDtypeStruct((nx, ny, nz), F32),
        scratch_shapes=[pltpu.VMEM((xb + 6, ny, nz), F32)]
        + [pltpu.VMEM((unroll, halves, ny + 16, 128), F32)] * 2
        + [pltpu.VMEM((unroll * ny, 2 * nz), BF16)] * 2,
        input_output_aliases={} if after is None else {0: 0},
        compiler_params=params(1),
        cost_estimate=cost(12 * count * xb * ny * nz * nz, 12 * count * xb * ny * nz),
        name="stencil_outer" if outer else "stencil_inner",
    )(weighted if after is None else after, *bands, *extra, weighted, weighted, weighted, residual)


def stencil_sides(partial, where, bands, edges, corners):
    nx, ny, nz = partial.shape

    rows, cols = lax.axis_size("row"), lax.axis_size("col")

    def kernel(where_ref, bh, bl, ea, ec, ca, cc, r_ref, out, ext, ph, qh):
        me, mine = where_ref[0], where_ref[1]
        for side in range(2):

            @pl.when(pl.program_id(0) == side)
            def _():
                ph[...] = jnp.zeros_like(ph)
                qh[...] = jnp.zeros_like(qh)
                base = 5 if side == 0 else 16
                near = mine % 2 == 1 - side
                pick = jnp.where(near, 0, 1)
                border = mine == (0 if side == 0 else cols - 1)
                for j in range(3):
                    edge = jnp.where(near, ea[j], ec[j])
                    even = me % 2 == 0
                    low = jnp.where(even, cc[pick, j], ca[pick, j])
                    high = jnp.where(even, ca[pick, j], cc[pick, j])
                    ext[:8] = jnp.where(border | (me == 0), 0.0, low)
                    ext[8 : 8 + nx] = jnp.where(border, 0.0, edge)
                    ext[8 + nx :] = jnp.where(border | (me == rows - 1), 0.0, high)
                    p, q = taps(lambda o: ext[8 + o : 8 + o + nx, :])
                    ph[:, base + j, :] = p
                    qh[:, base + j, :] = q

        @pl.loop(0, nx // 16)
        def _(g):
            at = pl.ds(16 * g, 16)
            mp, kp = taps(lambda o: ph[at, 8 + o : 16 + o, :])
            (mq,) = taps(lambda o: qh[at, 8 + o : 16 + o, :], stiff=False)
            both = split(jnp.concatenate([kp + mq, mp], 2).reshape(128, 2 * nz))
            image = dot3(both, (bh[...], bl[...]), NN)
            out[at] = r_ref[at] - image.reshape(16, 8, nz)

    field = pl.BlockSpec((nx, 8, nz), lambda i: (0, i * (ny // 8 - 1), 0))
    return pl.pallas_call(
        kernel,
        grid=(2,),
        in_specs=[pl.BlockSpec(memory_space=pltpu.SMEM)]
        + [whole(b.shape) for b in bands]
        + [whole(e.shape) for e in edges]
        + [whole(c.shape) for c in corners]
        + [field],
        out_specs=field,
        out_shape=jax.ShapeDtypeStruct((nx, ny, nz), F32),
        scratch_shapes=[pltpu.VMEM((nx + 16, nz), F32)]
        + [pltpu.VMEM((nx, 24, nz), F32)] * 2,
        input_output_aliases={7: 0},
        compiler_params=params(1),
        cost_estimate=cost(12 * nx * 16 * nz * nz, 128 * nx * nz),
        name="stencil_sides",
    )(where, *bands, *edges, *corners, partial)


def exchange(pieces, axis):
    n = len(pieces)
    out = [pieces[0]] + [None] * (n - 1)
    for d in range(n - 1, 0, -1):
        out[d] = lax.ppermute(pieces[d], axis, [(i, i ^ d) for i in range(n)])
    return out


def swap(array, axis, near):
    n = lax.axis_size(axis)
    other = [i ^ 1 if near else (i + 1 if i % 2 else i - 1) for i in range(n)]
    return lax.ppermute(
        array, axis, [(i, j if 0 <= j < n else i) for i, j in enumerate(other)]
    )


def schedule(chunks):
    order = [("z", 0), ("z", 1)][:chunks]
    if chunks == 4:
        order += [("x", 0), ("y", 0), ("x", 1), ("b", 0), ("y", 1), ("x", 2)]
        order += [("b", 1), ("y", 2), ("x", 3), ("b", 2), ("y", 3), ("b", 3)]
    else:
        order += [(s, k) for k in range(chunks) for s in ("x", "y", "b")]
    return order


def cut_count(nx):
    return 2 if nx % 16 == 0 and nx // 8 >= 6 else 1


def chunk_count(nz, rows):
    return max(1, min(4, nz // (rows * 8)))


def shards(residual, adjoint, coefficient, basis_x, basis_y, basis_z, eigen_x, eigen_y, eigen_z):
    nx, ny, nz = residual.shape
    rows, cols = lax.axis_size("row"), lax.axis_size("col")
    ri, ci = lax.axis_index("row"), lax.axis_index("col")
    width_x = nx * rows
    wide = width_x // cols
    chunks = chunk_count(nz, rows)
    part = nz // (rows * chunks)
    where = jnp.stack([ri, ci]).astype(jnp.int32)
    steps = nx // 8
    cuts = cut_count(nx)

    basis_zt = basis_z.T
    bx = jnp.concatenate(
        [lax.dynamic_slice_in_dim(basis_x, (ri ^ d) * nx, nx, 0) for d in range(rows)], 0
    )
    bx = jnp.concatenate(
        [lax.dynamic_slice_in_dim(bx, (ci ^ e) * wide, wide, 1) for e in range(cols)], 1
    )
    by = jnp.concatenate(
        [lax.dynamic_slice_in_dim(basis_y, (ci ^ e) * ny, ny, 0) for e in range(cols)], 0
    )
    bx2, by2 = split_outside(bx), split_outside(by)
    bxt2, byt2 = tuple(b.T for b in bx2), tuple(b.T for b in by2)
    ex = lax.dynamic_slice_in_dim(eigen_x, ci * wide, wide)
    ez = lax.dynamic_slice_in_dim(eigen_z.reshape(chunks, rows, part), ri, 1, 1)[:, 0]
    shift = (ez[:, :, None] + ex[None, None, :])[..., None]
    ey = eigen_y[None, :]
    bands = split_outside(band(nz))

    fw, mid, ret, back = ([None] * chunks for _ in range(4))
    last = where
    for stage, k in schedule(chunks):
        if stage == "z":
            these = (k,) if k == 0 else tuple(range(k, chunks))
            outs = forward_z(residual, basis_zt, where, these, rows, part)
            for n, out in zip(these, outs):
                fw[n] = (out, "row")
            last = outs[-1][0]
        elif stage == "x":
            out = forward_x(fw[k], bxt2, cols, last)
        elif stage == "y":
            out = middle_y(mid[k], by2, byt2, shift[k], ey, last)
        else:
            parts = cuts if k == chunks - 1 else 1
            out = backward_x(ret[k], bx2, rows, last, parts)
        if stage == "z":
            fw[k] = exchange(*fw[k])
        elif stage == "x":
            mid[k] = exchange(out, "col")
        elif stage == "y":
            ret[k] = exchange(out, "col")
        else:
            back[k] = exchange(out[:rows], "row")
        if stage == "x" and k + 2 < chunks:
            fw[k + 2] = exchange(*fw[k + 2])
        if stage != "z":
            last = out[0]
    late = exchange(out[rows:], "row") if cuts > 1 else None
    fields = (basis_zt, where, adjoint, coefficient)
    if cuts > 1:
        early = backward_z(back, *fields, 0, cuts)
        begun = stencil(early[1], residual, bands, 1, steps // 2 - 2)
        back = back[:-1] + [late]
        done = backward_z(back, *fields, 1, cuts, (*early, begun))
        rest = (steps // 2 - 1, steps // 2)
    else:
        done = backward_z(back, *fields)
        begun, rest = None, (1, steps - 2)
    adjoint_next, weighted, ea, ec, xa, xc = done
    ea, ec = swap(ea, "col", True), swap(ec, "col", False)
    xa, xc = swap(xa, "row", True), swap(xc, "row", False)
    inner = stencil(weighted, residual, bands, *rest, after=begun)
    sides, _ = lax.optimization_barrier((jnp.stack([ea, ec]), inner))
    low, high = sides[:, :, :8], sides[:, :, -8:]
    even = ri % 2 == 0
    ca = swap(jnp.where(even, high, low), "row", True)
    cc = swap(jnp.where(even, low, high), "row", False)
    outer = stencil(weighted, residual, bands, halos=(where, xa, xc), after=inner)
    residual_next = stencil_sides(outer, where, bands, (ea, ec), (ca, cc))
    return adjoint_next, residual_next


def solution(mesh):
    field = P("row", "col", None)
    return jax.shard_map(
        shards,
        mesh=mesh,
        in_specs=(field,) * 3 + (P(),) * 6,
        out_specs=(field, field),
        check_vma=False,
    )
```
